32 devices in a mesh: grp: 2 (over x), tm: 16 (over z, y, core).
Axes of the slice: x: 2, y: 2, z: 4, core: 2. Of those that a mesh axis runs over, the one named last changes fastest.
Arguments:
- transformer_tiles: float32 [6144, 128], P(('grp', 'tm')), parts along dimension 0, may hold values from -6 to 6
- global_tile_index: int32 [32, 192], P(('grp', 'tm')), parts along dimension 0, may hold values from 0 to 3071, as said below
- video_frame_count: int32 [16], P('grp'), parts along dimension 0, may hold values from 1 to 16, 64 in all
- input_conv_weight: float32 [3, 144, 384], replicated, may hold values from -0.3125 to 0.3125
- input_conv_bias: float32 [384], replicated, may hold values from -3 to 3
- first_norm_gain: float32 [384], replicated, may hold values from 0.1 to 1.9
- residual_conv_weight: bfloat16 [3, 3456, 384], replicated, may hold values from -0.0625 to 0.0625
- residual_conv_bias: float32 [384], replicated, may hold values from -3 to 3
- second_norm_gain: float32 [384], replicated, may hold values from 0.1 to 1.9
Outputs:
- block_input: bfloat16 [128, 16, 24, 384], P(('grp', 'tm')), parts along dimension 0
- branch_act: bfloat16 [128, 16, 24, 384], P(('grp', 'tm')), parts along dimension 0
The draws below stay inside these ranges and needn't reach their ends.
There are 2 independent parts, one for each index of `grp`. The reference program is written for one: setup_inputs(seed, part) draws one part's arguments, and reference() takes and returns one part's arrays. A program takes and returns all parts, laid end to end along the dimension named above; an argument that names none is the same for every part. Nothing has to cross between parts.
Inputs may be any that keep to these rules, and one draw needn't show every extreme that they name: `global_tile_index`: entry (j, i) is the id receiver * 192 + slot of the i-th tile that DiT owner j stores; every id of 0 to 3071 appears exactly once; an owner holds at most 24 tiles of any one receiver, and in every draw some owners hold exactly 24 of one receiver. Slot s of receiver r is latent frame r * 4 + s // 48, row (s // 3) % 16, columns 8 (s % 3) onward. `video_frame_count`: the counts sum to 64; the longest video has exactly 16 frames.
All inputs are finite; a program needn't handle non-finite values.
Results may differ from the reference program's by a relative error of at most 0.0054.
Values may be sent and summed in bfloat16 or wider, within the bound.
No kernel may reach another device: no remote copies, remote signals or barrier semaphores. Data moves between devices by JAX's collectives and lax.ppermute only.
A program may use at most 64 MiB of HBM per device.

```python
import math
import jax
import jax.numpy as jnp
import numpy as np
from jax import lax

LATENT_CHANNELS = 16
C = 384
HL = 16
WL = 24
VIDEOS = 8
TIME_BLOCKS = 16
T_LAT = 64
MOST_LEN = 16
DEVICE_TILES = 192
CAP = 24


def draw_global_tile_index(key, part):
    offsets = jax.random.permutation(jax.random.fold_in(key, 11), TIME_BLOCKS).astype(jnp.int32)
    senders = jax.random.permutation(jax.random.fold_in(key, 12), TIME_BLOCKS).astype(jnp.int32)
    receivers = jax.random.permutation(jax.random.fold_in(key, 13), TIME_BLOCKS).astype(jnp.int32)
    slot_keys = jax.random.split(jax.random.fold_in(key, 14), TIME_BLOCKS)
    slot_perm = jax.vmap(lambda sub_key: jax.random.permutation(sub_key, DEVICE_TILES))(slot_keys).astype(jnp.int32)
    order_keys = jax.random.split(jax.random.fold_in(key, 15), TIME_BLOCKS)
    storage = jax.vmap(lambda sub_key: jax.random.permutation(sub_key, DEVICE_TILES))(order_keys).astype(jnp.int32)
    full_groups = DEVICE_TILES // CAP - 1
    leftover = DEVICE_TILES - CAP * full_groups
    queue = jnp.arange(DEVICE_TILES, dtype=jnp.int32)
    groups = jnp.where(queue < full_groups * CAP, queue // CAP, jnp.where(queue < full_groups * CAP + leftover // 2, full_groups, full_groups + 1))
    sender_rank = jnp.argsort(senders).astype(jnp.int32)
    receiver = receivers[(sender_rank[:, None] - offsets[groups][None, :]) % TIME_BLOCKS]
    slots = slot_perm[receiver, queue[None, :]]
    tile_ids = receiver * DEVICE_TILES + slots
    return jnp.take_along_axis(tile_ids, storage, axis=1).astype(jnp.int32)


def steps_of(rng, extent, cuts, low, top_value):
    gain = 1.0
    for position, parts in cuts:
        heights = jax.random.uniform(jax.random.fold_in(jax.random.fold_in(rng, 6), position), (parts,), jnp.float32, low / len(cuts), top_value / len(cuts))
        gain = gain * jnp.repeat(jnp.exp(heights), extent[position] // parts).reshape((-1,) + (1,) * (len(extent) - 1 - position))
    return gain


def profile(number_of, total, bound, skew):
    loads = [(1 << 20) // math.isqrt(standing ** skew) + 1 for standing in range(2, number_of + 1)]
    rest, given = total - bound - (number_of - 1), [1] * (number_of - 1)
    while rest > 0:
        movable = [i for i in range(number_of - 1) if given[i] < bound]
        pool, left = sum([loads[i] for i in movable]), rest
        for i in movable:
            extra = min(bound - given[i], max(1, left * loads[i] // pool), rest)
            given[i] = given[i] + extra
            rest = rest - extra
    return np.array([bound] + given)


def uneven(key, number_of, total, limit, slope):
    if number_of == 2:
        one = jax.random.randint(key, (), max(1, total - limit), min(limit, total - 1) + 1)
        return jnp.stack([one, total - one])
    lengths = jnp.asarray(profile(number_of, total, limit, slope), jnp.int32)
    twos = (number_of - 1) // 2
    source_of, taker = lengths[1:1 + 2 * twos:2], lengths[2:2 + 2 * twos:2]
    margin = jnp.minimum(source_of - 1, limit - taker)
    passed = jax.random.randint(jax.random.fold_in(key, 1), (twos,), 0, 1 << 20) % (margin + 1)
    lengths = lengths.at[1:1 + 2 * twos:2].set(source_of - passed).at[2:2 + 2 * twos:2].set(taker + passed)
    return lengths[jax.random.permutation(jax.random.fold_in(key, 2), number_of)]


def scatter_about(rng, extent, scale, reach, pieces=(), kind=jnp.bfloat16):
    result = jax.random.normal(rng, extent, jnp.float32) * scale
    if len(pieces) > 0:
        result = steps_of(rng, extent, pieces, -0.22, 0.18) * result
    return jnp.clip(result, min=-reach, max=reach).astype(kind)


def setup_inputs(seed: int = 0, part: int = 0) -> dict:
    arg_keys = jax.random.split(jax.random.key(seed), 10)
    own_keys = jax.random.split(jax.random.fold_in(arg_keys[9], part), 10)
    return {
        "transformer_tiles": scatter_about(own_keys[0], (TIME_BLOCKS * DEVICE_TILES, 8 * LATENT_CHANNELS), 1.0, 6.0, ((0, 16),), jnp.float32),
        "global_tile_index": draw_global_tile_index(jax.random.fold_in(jax.random.fold_in(arg_keys[9], part), 71), part),
        "video_frame_count": uneven(own_keys[2], VIDEOS, T_LAT, MOST_LEN, 2).astype(jnp.int32),
        "input_conv_weight": scatter_about(arg_keys[3], (3, 9 * LATENT_CHANNELS, C), (27 * LATENT_CHANNELS) ** -0.5, 0.3125, (), jnp.float32),
        "input_conv_bias": scatter_about(arg_keys[4], (C,), 0.5, 3.0, (), jnp.float32),
        "first_norm_gain": jnp.clip(1.0 + 0.18 * jax.random.normal(arg_keys[5], (C,), jnp.float32), 0.1, 1.9),
        "residual_conv_weight": scatter_about(arg_keys[6], (3, 9 * C, C), (27 * C) ** -0.5, 0.0625),
        "residual_conv_bias": scatter_about(arg_keys[7], (C,), 0.5, 3.0, (), jnp.float32),
        "second_norm_gain": jnp.clip(1.0 + 0.18 * jax.random.normal(arg_keys[8], (C,), jnp.float32), 0.1, 1.9),
    }


def frame_masks(video_frame_count, frames):
    bounds = (jnp.cumsum(video_frame_count) - video_frame_count).astype(jnp.int32)
    starts = lax.optimization_barrier(jnp.max(jnp.where(bounds[None, :] <= frames[:, None], bounds[None, :], 0), axis=1))
    lag_one = (frames - 1 >= starts).astype(jnp.float32)
    lag_two = (frames - 2 >= starts).astype(jnp.float32)
    return (lag_one, lag_two)

def causal_conv(values, weight, lag_one, lag_two, precision):
    chan_in = values.shape[-1]
    chan_out = weight.shape[-1]
    results = []
    for lag_step in range(3):
        kernel = weight[lag_step].reshape(3, 3, chan_in, chan_out)
        results.append(lax.conv_general_dilated(values, kernel, (1, 1), ((1, 1), (1, 1)), dimension_numbers=('NHWC', 'HWIO', 'NHWC'), precision=precision))
    shift_one = jnp.pad(results[1], ((1, 0), (0, 0), (0, 0), (0, 0)))[:-1]
    shift_two = jnp.pad(results[2], ((2, 0), (0, 0), (0, 0), (0, 0)))[:-2]
    return results[0] + lag_one[:, None, None, None] * shift_one + lag_two[:, None, None, None] * shift_two

def activate(values, scale_gain):
    normed = values * lax.rsqrt(lax.optimization_barrier(jnp.mean(values * values, axis=-1, keepdims=True)) + 1e-06)
    return jax.nn.silu(normed * scale_gain)

def reference(transformer_tiles, global_tile_index, video_frame_count, input_conv_weight, input_conv_bias, first_norm_gain, residual_conv_weight, residual_conv_bias, second_norm_gain):
    placed_tiles = jnp.zeros_like(transformer_tiles).at[global_tile_index.reshape(-1)].set(transformer_tiles)
    latent = placed_tiles.reshape(T_LAT, HL, WL, LATENT_CHANNELS)
    frames = jnp.arange(T_LAT, dtype=jnp.int32)
    lag_one, lag_two = frame_masks(video_frame_count, frames)
    pre_one = causal_conv(latent, input_conv_weight, lag_one, lag_two, lax.Precision.HIGHEST) + input_conv_bias
    block_input = pre_one.astype(jnp.bfloat16)
    act_one = activate(block_input.astype(jnp.float32), first_norm_gain).astype(jnp.bfloat16)
    pre_two = causal_conv(act_one.astype(jnp.float32), residual_conv_weight.astype(jnp.float32), lag_one, lag_two, None) + residual_conv_bias
    branch_act = activate(pre_two, second_norm_gain).astype(jnp.bfloat16)
    return (block_input, branch_act)
```

```python
import functools

import jax
import jax.numpy as jnp
from jax import lax
from jax.experimental import pallas as pl
from jax.experimental.pallas import tpu as pltpu
from jax.sharding import PartitionSpec as P

CH = 16
C = 384
LT = 4
HL = 16
WL = 24
TILE_X = 8
ROWS = HL * WL // TILE_X
PIX = HL * WL
HALO = 2
NF = LT + HALO
K2 = 9 * C
F32 = jnp.float32
BF16 = jnp.bfloat16


def iota(shape, dim):
    return lax.broadcasted_iota(jnp.int32, shape, dim)


def fdiv(x, n):
    return jnp.floor((x + 0.5) * (1.0 / n))


def chunk_sizes(n, tiles):
    cap = max(2, 2 * tiles // n)
    rows = 8
    while rows < 2 * cap + 1:
        rows *= 2
    return cap, rows


def pack_kernel(n, cap, rows, tiles_ref, idx_ref, out_ref):
    tiles = tiles_ref.shape[0]
    ids = idx_ref[...].astype(F32)
    r_row = fdiv(ids, tiles)
    s_row = ids - r_row * tiles
    sub = iota((tiles, tiles), 0)
    lane = iota((tiles, tiles), 1)
    r_col = jnp.sum(jnp.where(sub == lane, r_row, 0.0), axis=1, keepdims=True)
    same = r_col == r_row
    rank_row = jnp.sum(jnp.where(same & (sub < lane), 1.0, 0.0), axis=0, keepdims=True)
    rank_col = jnp.sum(jnp.where(same & (lane < sub), 1.0, 0.0), axis=1, keepdims=True)
    pos_row = r_row * cap + rank_row
    rho = iota((n * rows, 1), 0).astype(F32)
    d = fdiv(rho, rows)
    q = rho - d * rows
    key = jnp.where(q < cap, d * cap + q, jnp.where(q < 2 * cap, (d - 1.0) * cap + q - cap, -1.0))
    onehot = (key == pos_row).astype(F32).astype(BF16)
    moved = jnp.dot(onehot, tiles_ref[...].astype(BF16), preferred_element_type=F32)
    dev = iota((n, 1), 0).astype(F32)
    slot1 = s_row + 1.0
    a_own = jnp.where(dev == r_row, slot1, 0.0).astype(BF16)
    a_prev = jnp.where(dev - 1.0 == r_row, slot1, 0.0).astype(BF16)
    offset = lax.rem(lax.axis_index("tm"), 128 // rows) * rows
    place = iota((tiles, 128), 1) - offset
    rank_i = rank_col.astype(jnp.int32)
    b_own = (place == rank_i).astype(F32).astype(BF16)
    b_prev = (place - cap == rank_i).astype(F32).astype(BF16)
    id_rows = jnp.dot(a_own, b_own, preferred_element_type=F32) + jnp.dot(
        a_prev, b_prev, preferred_element_type=F32
    )
    q3 = iota((n, rows, 128), 1)
    full = jnp.where(q3 == 2 * cap, id_rows[:, None, :], moved.reshape(n, rows, 128))
    out_ref[...] = full.astype(BF16).reshape(n * rows, 128)


def activate(values, gain):
    ms = jnp.mean(values * values, axis=-1, keepdims=True)
    scaled = values * lax.rsqrt(ms + 1e-06) * gain
    return scaled / (1.0 + jnp.exp(-scaled))


def decode_kernel(
    cap,
    rows,
    vfc_ref,
    inc_ref,
    wp_ref,
    b1_ref,
    g1_ref,
    w2_ref,
    b2_ref,
    g2_ref,
    bi_ref,
    ba_ref,
    w2v,
    win,
    lhs,
    pre,
    actf,
    cols,
    acc,
    sem,
):
    for tap in range(3):
        pltpu.make_async_copy(w2_ref.at[tap], w2v.at[:, pl.ds(tap * C, C)], sem.at[tap]).start()
    first = lax.axis_index("tm") * LT
    starts = [jnp.int32(0)] * NF
    bound = jnp.int32(0)
    for v in range(vfc_ref.shape[0]):
        for f in range(NF):
            starts[f] = jnp.where(bound <= first - HALO + f, bound, starts[f])
        bound = bound + vfc_ref[v]
    lags = []
    for f in range(NF):
        t = first - HALO + f
        lags.append(
            [
                None,
                jnp.where(t - 1 >= starts[f], 1.0, 0.0).astype(F32),
                jnp.where(t - 2 >= starts[f], 1.0, 0.0).astype(F32),
            ]
        )
    total = inc_ref.shape[0]
    groups = total // 128
    inc = inc_ref[...]
    k_idx = iota((8, total), 1)
    sel = (lax.rem(k_idx, rows) == 2 * cap) & (lax.div(k_idx, 128) == iota((8, total), 0))
    ids = jnp.dot(sel.astype(F32).astype(BF16), inc, preferred_element_type=F32)
    place = lax.rem(iota((1, 128), 1), rows)
    half = LT * ROWS
    slot1 = (iota((half, 1), 0) + 1).astype(F32)
    pieces = []
    for g in range(groups):
        id_g = ids[g : g + 1, :]
        own = jnp.where(place < cap, id_g, 0.0)
        prev = jnp.where((place >= cap) & (place < 2 * cap), id_g, 0.0)
        hit = jnp.concatenate([slot1 == prev, slot1 == own], axis=0)
        pieces.append(hit.astype(F32).astype(BF16))
    tiles = jnp.dot(jnp.concatenate(pieces, axis=1), inc, preferred_element_type=F32)
    n_rows = 2 * half
    rho = iota((n_rows, 1), 0).astype(F32)
    in_frame = rho - fdiv(rho, ROWS) * ROWS
    h = fdiv(in_frame, WL // TILE_X)
    xt = in_frame - h * (WL // TILE_X)
    lane = iota((n_rows, 128), 1)
    step = WL // TILE_X
    for a in range(3):
        if a == 0:
            pa = jnp.where(h >= 1, pltpu.roll(tiles, step, 0), 0.0)
        elif a == 1:
            pa = tiles
        else:
            pa = jnp.where(h <= HL - 2, pltpu.roll(tiles, n_rows - step, 0), 0.0)
        left = jnp.where(xt >= 1, pltpu.roll(pa, 1, 0), 0.0)
        right = jnp.where(xt <= step - 2, pltpu.roll(pa, n_rows - 1, 0), 0.0)
        y = jnp.where(lane < CH, pltpu.roll(left, CH, 1), pltpu.roll(pa, CH, 1))
        z = jnp.where(lane < 3 * CH, pltpu.roll(pa, 3 * CH, 1), pltpu.roll(right, 3 * CH, 1))
        win[a, 0] = y
        win[a, 1] = pltpu.roll(y, 96, 1)
        win[a, 2] = pltpu.roll(y, 64, 1)
        win[a, 3] = pltpu.roll(y, 32, 1)
        win[a, 4] = z
        win[a, 5] = pltpu.roll(z, 64, 1)
    low = (0, 1, 2, 4)
    high = (2, 3, 0, 5)
    lane48 = iota((ROWS, 128), 1)

    def tap_rows(tap, which, f):
        d, a = divmod(tap, 3)
        value = win[a, which, pl.ds((f + HALO - d) * ROWS, ROWS), :]
        return value if d == 0 else value * lags[f][d]

    for p in range(4):
        for f in range(NF):
            for m in range(5):
                value = tap_rows(2 * m, low[p], f)
                if m < 4:
                    value = jnp.where(lane48 < 64, value, tap_rows(2 * m + 1, high[p], f))
                lhs[p, pl.ds(f * ROWS, ROWS), pl.ds(m * 128, 128)] = value.astype(BF16)
    for p in range(4):
        out = jnp.dot(lhs[p, :, : 9 * 64], wp_ref[...], preferred_element_type=F32)
        for j in range(2 * C // 128):
            x_col, m = 2 * p + j // 3, j % 3
            pre[m, pl.ds(x_col, NF * ROWS, stride=TILE_X), :] = out[:, j * 128 : (j + 1) * 128]
    pix = iota((PIX, 1), 0).astype(F32)
    x = pix - fdiv(pix, WL) * WL
    for tap in range(3):
        pltpu.make_async_copy(w2_ref.at[tap], w2v.at[:, pl.ds(tap * C, C)], sem.at[tap]).wait()
    for f in range(NF):
        raw = jnp.concatenate([pre[m, pl.ds(f * PIX, PIX), :] for m in range(3)], axis=1)
        block = (raw + b1_ref[...]).astype(BF16)
        if f >= HALO:
            bi_ref[pl.ds((f - HALO) * PIX, PIX), :] = block
        actf[pl.ds(8, PIX), :] = activate(block.astype(F32), g1_ref[...])
        slot = f % 2
        for b in range(3):
            value = actf[pl.ds(7 + b, PIX), :]
            if b == 0:
                value = jnp.where(x >= 1, value, 0.0)
            elif b == 2:
                value = jnp.where(x <= WL - 2, value, 0.0)
            edge = jnp.zeros((WL, C), F32)
            up = jnp.concatenate([edge, value[:-WL]], axis=0)
            down = jnp.concatenate([value[WL:], edge], axis=0)
            for a, part in enumerate((up, value, down)):
                cols[slot, :, pl.ds((3 * a + b) * C, C)] = part.astype(BF16)
        taps = [d for d in range(3) if 0 <= f - HALO + d < LT]
        prod = jnp.dot(
            cols[slot], w2v[:, taps[0] * C : (taps[-1] + 1) * C], preferred_element_type=F32
        )
        for i, d in enumerate(taps):
            o = f - HALO + d
            part = prod[:, i * C : (i + 1) * C]
            if d > 0:
                part = part * lags[o + HALO][d]
            if d == 2:
                acc[o] = part
            elif d == 1:
                acc[o] += part
            else:
                value = acc[o] + part + b2_ref[...]
                ba_ref[pl.ds(o * PIX, PIX), :] = activate(value, g2_ref[...]).astype(BF16)


def pair_weights(w1):
    taps = w1.reshape(3, 3, 3, CH, C)
    even = jnp.pad(taps, ((0, 0), (0, 0), (0, 1), (0, 0), (0, 0)))
    odd = jnp.pad(taps, ((0, 0), (0, 0), (1, 0), (0, 0), (0, 0)))
    return jnp.concatenate([even, odd], axis=-1).reshape(9 * 64, 2 * C).astype(BF16)


def local(
    transformer_tiles,
    global_tile_index,
    video_frame_count,
    input_conv_weight,
    input_conv_bias,
    first_norm_gain,
    residual_conv_weight,
    residual_conv_bias,
    second_norm_gain,
):
    n = lax.axis_size("tm")
    cap, rows = chunk_sizes(n, transformer_tiles.shape[0])
    vmem = pl.BlockSpec(memory_space=pltpu.VMEM)
    smem = pl.BlockSpec(memory_space=pltpu.SMEM)
    hbm = pl.BlockSpec(memory_space=pl.ANY)
    outbound = pl.pallas_call(
        functools.partial(pack_kernel, n, cap, rows),
        out_shape=jax.ShapeDtypeStruct((n * rows, 128), BF16),
        in_specs=[vmem, vmem],
        out_specs=vmem,
        name="pack",
    )(transformer_tiles, global_tile_index)
    incoming = lax.all_to_all(
        outbound.reshape(n, rows, 128), "tm", split_axis=0, concat_axis=0, tiled=True
    ).reshape(n * rows, 128)
    half = LT * ROWS
    block_input, branch_act = pl.pallas_call(
        functools.partial(decode_kernel, cap, rows),
        out_shape=[jax.ShapeDtypeStruct((LT * PIX, C), BF16)] * 2,
        in_specs=[smem, vmem, vmem, vmem, vmem, hbm, vmem, vmem],
        out_specs=[vmem, vmem],
        scratch_shapes=[
            pltpu.VMEM((K2, 3 * C), BF16),
            pltpu.VMEM((3, 6, 2 * half, 128), F32),
            pltpu.VMEM((4, NF * ROWS, 640), BF16),
            pltpu.VMEM((3, NF * PIX, 128), F32),
            pltpu.VMEM((PIX + 16, C), F32),
            pltpu.VMEM((2, PIX, K2), BF16),
            pltpu.VMEM((LT, PIX, C), F32),
            pltpu.SemaphoreType.DMA((3,)),
        ],
        compiler_params=pltpu.CompilerParams(vmem_limit_bytes=56 << 20),
        name="decode",
    )(
        video_frame_count,
        incoming,
        pair_weights(input_conv_weight),
        input_conv_bias.reshape(1, C),
        first_norm_gain.reshape(1, C),
        residual_conv_weight,
        residual_conv_bias.reshape(1, C),
        second_norm_gain.reshape(1, C),
    )
    shape = (LT, HL, WL, C)
    return (block_input.reshape(shape), branch_act.reshape(shape))


def solution(mesh):
    placed = (
        P(("grp", "tm"), None),
        P(("grp", "tm"), None),
        P("grp"),
        P(),
        P(),
        P(),
        P(),
        P(),
        P(),
    )
    return jax.shard_map(
        local,
        mesh=mesh,
        in_specs=placed,
        out_specs=(P(("grp", "tm"), None, None, None), P(("grp", "tm"), None, None, None)),
        check_vma=False,
    )
```

```python
import functools

import jax
import jax.numpy as jnp
from jax import lax
from jax.experimental import pallas as pl
from jax.experimental.pallas import tpu as pltpu
from jax.sharding import PartitionSpec as P

CH = 16
C = 384
LT = 4
HL = 16
WL = 24
TILE_X = 8
ROWS = HL * WL // TILE_X
PIX = HL * WL
HALO = 2
NF = LT + HALO
K2 = 9 * C
F32 = jnp.float32
BF16 = jnp.bfloat16


def iota(shape, dim):
    return lax.broadcasted_iota(jnp.int32, shape, dim)


def fdiv(x, n):
    return jnp.floor((x + 0.5) * (1.0 / n))


def chunk_sizes(n, tiles):
    cap = max(2, 2 * tiles // n)
    sent = (2 * cap + 8) // 8 * 8
    rows = 8
    while rows < sent:
        rows *= 2
    return cap, sent, rows


def pack_kernel(n, cap, sent, rows, tiles_ref, idx_ref, out_ref):
    tiles = tiles_ref.shape[0]
    ids = idx_ref[...].astype(F32)
    r_row = fdiv(ids, tiles)
    s_row = ids - r_row * tiles
    sub = iota((tiles, tiles), 0)
    lane = iota((tiles, tiles), 1)
    r_col = jnp.sum(jnp.where(sub == lane, r_row, 0.0), axis=1, keepdims=True)
    same = r_col == r_row
    rank_row = jnp.sum(jnp.where(same & (sub < lane), 1.0, 0.0), axis=0, keepdims=True)
    rank_col = jnp.sum(jnp.where(same & (lane < sub), 1.0, 0.0), axis=1, keepdims=True)
    pos_row = r_row * cap + rank_row
    rho = iota((n * sent, 1), 0).astype(F32)
    d = fdiv(rho, sent)
    q = rho - d * sent
    key = jnp.where(q < cap, d * cap + q, jnp.where(q < 2 * cap, (d - 1.0) * cap + q - cap, -1.0))
    onehot = (key == pos_row).astype(F32).astype(BF16)
    moved = jnp.dot(onehot, tiles_ref[...].astype(BF16), preferred_element_type=F32)
    dev = iota((n, 1), 0).astype(F32)
    slot1 = s_row + 1.0
    a_own = jnp.where(dev == r_row, slot1, 0.0).astype(BF16)
    a_prev = jnp.where(dev - 1.0 == r_row, slot1, 0.0).astype(BF16)
    offset = lax.rem(lax.axis_index("tm"), 128 // rows) * rows
    place = iota((tiles, 128), 1) - offset
    rank_i = rank_col.astype(jnp.int32)
    b_own = (place == rank_i).astype(F32).astype(BF16)
    b_prev = (place - cap == rank_i).astype(F32).astype(BF16)
    id_rows = jnp.dot(a_own, b_own, preferred_element_type=F32) + jnp.dot(
        a_prev, b_prev, preferred_element_type=F32
    )
    q3 = iota((n, sent, 128), 1)
    full = jnp.where(q3 == 2 * cap, id_rows[:, None, :], moved.reshape(n, sent, 128))
    out_ref[...] = full.astype(BF16)


def prep_kernel(w1_ref, wp_ref):
    zero = jnp.zeros((CH, C), BF16)
    for d in range(3):
        for a in range(3):
            for c in range(4):
                for j in range(2):
                    rows = pl.ds((3 * d + a) * 64 + c * CH, CH)
                    inside = 0 <= c - j < 3
                    value = w1_ref[d, pl.ds((3 * a + c - j) * CH, CH), :].astype(BF16) if inside else zero
                    wp_ref[rows, pl.ds(j * C, C)] = value


def activate(values, gain):
    ms = jnp.mean(values * values, axis=-1, keepdims=True)
    scaled = values * lax.rsqrt(ms + 1e-06) * gain
    return scaled / (1.0 + jnp.exp(-scaled))


def decode_kernel(
    cap,
    vfc_ref,
    inc_ref,
    wp_ref,
    b1_ref,
    g1_ref,
    w2_ref,
    b2_ref,
    g2_ref,
    bi_ref,
    ba_ref,
    inc_v,
    w2v,
    win,
    lhs,
    pre,
    actf,
    cols_even,
    cols_odd,
    acc,
    bi_v,
    ba_v,
    sem,
):
    n, sent, _ = inc_ref.shape
    cols = (cols_even, cols_odd)
    rows = inc_v.shape[1]
    fetch = pltpu.make_async_copy(inc_ref, inc_v.at[:, pl.ds(0, sent), :], sem.at[0])
    fetch.start()

    def load(tap):
        return pltpu.make_async_copy(
            w2_ref.at[tap], w2v.at[:, pl.ds(tap * C, C)], sem.at[1 + 2 * LT + tap]
        )

    for tap in (2, 1, 0):
        load(tap).start()
    if rows > sent:
        inc_v[:, sent:, :] = jnp.zeros((n, rows - sent, 128), BF16)

    def send(source, target, o, first_sem):
        return pltpu.make_async_copy(
            source.at[o], target.at[pl.ds(o * PIX, PIX), :], sem.at[first_sem + o]
        )

    bias1, gain1 = b1_ref[...].reshape(1, C), g1_ref[...].reshape(1, C)
    bias2, gain2 = b2_ref[...].reshape(1, C), g2_ref[...].reshape(1, C)
    first = lax.axis_index("tm") * LT
    starts = [jnp.int32(0)] * NF
    bound = jnp.int32(0)
    for v in range(vfc_ref.shape[0]):
        for f in range(NF):
            starts[f] = jnp.where(bound <= first - HALO + f, bound, starts[f])
        bound = bound + vfc_ref[v]
    lags = []
    for f in range(NF):
        t = first - HALO + f
        lags.append(
            [
                None,
                jnp.where(t - 1 >= starts[f], 1.0, 0.0).astype(F32),
                jnp.where(t - 2 >= starts[f], 1.0, 0.0).astype(F32),
            ]
        )
    total = n * rows
    groups = total // 128
    fetch.wait()
    inc = inc_v[...].reshape(total, 128)
    k_idx = iota((8, total), 1)
    sel = (lax.rem(k_idx, rows) == 2 * cap) & (lax.div(k_idx, 128) == iota((8, total), 0))
    ids = jnp.dot(sel.astype(F32).astype(BF16), inc, preferred_element_type=F32)
    place = lax.rem(iota((1, 128), 1), rows)
    half = LT * ROWS
    slot1 = (iota((half, 1), 0) + 1).astype(F32)
    pieces = []
    for g in range(groups):
        id_g = ids[g : g + 1, :]
        own = jnp.where(place < cap, id_g, 0.0)
        prev = jnp.where((place >= cap) & (place < 2 * cap), id_g, 0.0)
        hit = jnp.concatenate([slot1 == prev, slot1 == own], axis=0)
        pieces.append(hit.astype(F32).astype(BF16))
    tiles = jnp.dot(jnp.concatenate(pieces, axis=1), inc, preferred_element_type=F32)
    n_rows = 2 * half
    step = WL // TILE_X
    rho = iota((n_rows, 1), 0).astype(F32)
    xt = rho - fdiv(rho, step) * step
    lane = iota((n_rows, 128), 1)
    left = jnp.where(xt >= 1, pltpu.roll(tiles, 1, 0), 0.0)
    right = jnp.where(xt <= step - 2, pltpu.roll(tiles, n_rows - 1, 0), 0.0)
    y = jnp.where(lane < CH, pltpu.roll(left, CH, 1), pltpu.roll(tiles, CH, 1))
    z = jnp.where(lane < 3 * CH, pltpu.roll(tiles, 3 * CH, 1), pltpu.roll(right, 3 * CH, 1))
    middle = pl.ds(8, n_rows)
    for k, value in enumerate(
        (y, pltpu.roll(y, 96, 1), pltpu.roll(y, 64, 1), pltpu.roll(y, 32, 1), z, pltpu.roll(z, 64, 1))
    ):
        win[k, pl.ds(0, 8), :] = jnp.zeros((8, 128), F32)
        win[k, pl.ds(8 + n_rows, 8), :] = jnp.zeros((8, 128), F32)
        win[k, middle, :] = value
    low = (0, 1, 2, 4)
    high = (2, 3, 0, 5)
    lane48 = iota((ROWS, 128), 1)
    row48 = iota((ROWS, 128), 0)
    inside = (
        jnp.where(row48 >= step, 1.0, 0.0),
        None,
        jnp.where(row48 < ROWS - step, 1.0, 0.0),
    )

    def tap_rows(tap, which, f):
        d, a = divmod(tap, 3)
        value = win[which, pl.ds(8 + (f + HALO - d) * ROWS + step * (a - 1), ROWS), :]
        if a != 1:
            value = value * inside[a]
        return value if d == 0 else value * lags[f][d]

    def lhs_piece(p, f):
        for m in range(5):
            value = tap_rows(2 * m, low[p], f)
            if m < 4:
                value = jnp.where(lane48 < 64, value, tap_rows(2 * m + 1, high[p], f))
            lhs[p, pl.ds(f * ROWS, ROWS), pl.ds(m * 128, 128)] = value.astype(BF16)

    def first_piece(p, f0, f1):
        rows_f = pl.ds(f0 * ROWS, (f1 - f0) * ROWS)
        out = jnp.dot(lhs[p, rows_f, : 9 * 64], wp_ref[...], preferred_element_type=F32)
        for j in range(2 * C // 128):
            x_col, m = 2 * p + j // 3, j % 3
            target = pl.ds(f0 * PIX + x_col, (f1 - f0) * ROWS, stride=TILE_X)
            pre[m, target, :] = out[:, j * 128 : (j + 1) * 128]

    act_rows = 32
    col_rows = 96
    pad = 32
    edge = jnp.zeros((pad, C), F32)
    actf[pl.ds(0, pad), :] = edge
    actf[pl.ds(pad + PIX, pad), :] = edge

    def act_piece(f, r):
        rows_r = pl.ds(f * PIX + r * act_rows, act_rows)
        raw = jnp.concatenate([pre[m, rows_r, :] for m in range(3)], axis=1)
        block = (raw + bias1).astype(BF16)
        if f >= HALO:
            bi_v[f - HALO, pl.ds(r * act_rows, act_rows), :] = block
        actf[pl.ds(pad + r * act_rows, act_rows), :] = activate(block.astype(F32), gain1)

    def cols_piece(f, r, m):
        target = cols[f % 2]
        lanes = pl.ds(m * 128, 128)
        pix = iota((col_rows, 128), 0).astype(F32)
        x = pix - fdiv(pix, WL) * WL
        for b in range(3):
            for a in range(3):
                source = pad + r * col_rows + (a - 1) * WL + b - 1
                value = actf[pl.ds(source, col_rows), lanes]
                if b != 1:
                    value = jnp.where(x >= 1 if b == 0 else x <= WL - 2, value, 0.0)
                at = pl.ds((3 * a + b) * C + m * 128, 128)
                target[pl.ds(r * col_rows, col_rows), at] = value.astype(BF16)

    def mxu_piece(f, taps, n0, width):
        start = taps[0] * C + n0
        prod = jnp.dot(
            cols[f % 2][...], w2v[:, start : start + width], preferred_element_type=F32
        )
        for t in range(width // 128):
            tile = n0 // 128 + t
            d, m = taps[tile // 3], tile % 3
            o = f - HALO + d
            part = prod[:, t * 128 : (t + 1) * 128]
            if d > 0:
                part = part * lags[o + HALO][d]
            if d == 2:
                acc[o, :, pl.ds(m * 128, 128)] = part
            else:
                acc[o, :, pl.ds(m * 128, 128)] += part

    def end_piece(o, r):
        rows_r = pl.ds(r * act_rows, act_rows)
        ba_v[o, rows_r, :] = activate(acc[o, rows_r, :] + bias2, gain2).astype(BF16)

    def end_work(o):
        return [functools.partial(end_piece, o, r) for r in range(PIX // act_rows)]

    def frame_work(f):
        work = [functools.partial(act_piece, f, r) for r in range(PIX // act_rows)]
        for r in range(PIX // col_rows):
            work += [functools.partial(cols_piece, f, r, m) for m in range(3)]
        return work

    def weave(work, pieces):
        given = 0
        for i, piece in enumerate(pieces):
            upto = len(work) * (i + 1) // len(pieces)
            for vector_piece in work[given:upto]:
                vector_piece()
            given = upto
            piece()

    early = HALO
    for p in range(4):
        for f in range(early):
            lhs_piece(p, f)
    weave(
        [functools.partial(lhs_piece, p, f) for p in range(4) for f in range(early, NF)],
        [functools.partial(first_piece, p, 0, early) for p in range(4)],
    )
    weave(frame_work(0), [functools.partial(first_piece, p, early, NF) for p in range(4)])
    for tap in (2, 1, 0):
        load(tap).wait()
    for f in range(NF):
        taps = [d for d in range(3) if 0 <= f - HALO + d < LT]
        width = len(taps) * C
        pieces = [
            functools.partial(mxu_piece, f, taps, n0, min(256, width - n0))
            for n0 in range(0, width, 256)
        ]
        work = end_work(f - 1 - HALO) if f > HALO else []
        if f + 1 < NF:
            work += frame_work(f + 1)
        weave(work, pieces)
        if f + 1 == NF - 1:
            for o in range(LT):
                send(bi_v, bi_ref, o, 1).start()
        if f + 1 >= NF - 1:
            for o in range(LT - 3, LT - 1) if f + 1 == NF else range(LT - 3):
                send(ba_v, ba_ref, o, 1 + LT).start()
    for piece in end_work(LT - 1):
        piece()
    send(ba_v, ba_ref, LT - 1, 1 + LT).start()
    for o in range(LT):
        send(bi_v, bi_ref, o, 1).wait()
        send(ba_v, ba_ref, o, 1 + LT).wait()


def local(
    transformer_tiles,
    global_tile_index,
    video_frame_count,
    input_conv_weight,
    input_conv_bias,
    first_norm_gain,
    residual_conv_weight,
    residual_conv_bias,
    second_norm_gain,
):
    n = lax.axis_size("tm")
    cap, sent, rows = chunk_sizes(n, transformer_tiles.shape[0])
    vmem = pl.BlockSpec(memory_space=pltpu.VMEM)
    smem = pl.BlockSpec(memory_space=pltpu.SMEM)
    hbm = pl.BlockSpec(memory_space=pl.ANY)
    outbound = pl.pallas_call(
        functools.partial(pack_kernel, n, cap, sent, rows),
        out_shape=jax.ShapeDtypeStruct((n, sent, 128), BF16),
        in_specs=[vmem, vmem],
        out_specs=vmem,
        name="pack",
    )(transformer_tiles, global_tile_index)
    incoming = lax.all_to_all(outbound, "tm", split_axis=0, concat_axis=0, tiled=True)
    pair_weights = pl.pallas_call(
        prep_kernel,
        out_shape=pltpu.VMEM((9 * 64, 2 * C), BF16),
        in_specs=[vmem],
        out_specs=vmem,
        compiler_params=pltpu.CompilerParams(vmem_limit_bytes=16 << 20),
        name="prep",
    )(input_conv_weight)
    half = LT * ROWS
    block_input, branch_act = pl.pallas_call(
        functools.partial(decode_kernel, cap),
        out_shape=[jax.ShapeDtypeStruct((LT * PIX, C), BF16)] * 2,
        in_specs=[smem, hbm, vmem, vmem, vmem, hbm, vmem, vmem],
        out_specs=[hbm, hbm],
        scratch_shapes=[
            pltpu.VMEM((n, rows, 128), BF16),
            pltpu.VMEM((K2, 3 * C), BF16),
            pltpu.VMEM((6, 2 * half + 16, 128), F32),
            pltpu.VMEM((4, NF * ROWS, 640), BF16),
            pltpu.VMEM((3, NF * PIX, 128), F32),
            pltpu.VMEM((PIX + 64, C), F32),
            pltpu.VMEM((PIX, K2), BF16),
            pltpu.VMEM((PIX, K2), BF16),
            pltpu.VMEM((LT, PIX, C), F32),
            pltpu.VMEM((LT, PIX, C), BF16),
            pltpu.VMEM((LT, PIX, C), BF16),
            pltpu.SemaphoreType.DMA((1 + 2 * LT + 3,)),
        ],
        compiler_params=pltpu.CompilerParams(vmem_limit_bytes=48 << 20),
        name="decode",
    )(
        video_frame_count,
        incoming,
        pair_weights,
        input_conv_bias,
        first_norm_gain,
        residual_conv_weight,
        residual_conv_bias,
        second_norm_gain,
    )
    shape = (LT, HL, WL, C)
    return (block_input.reshape(shape), branch_act.reshape(shape))


def solution(mesh):
    placed = (
        P(("grp", "tm"), None),
        P(("grp", "tm"), None),
        P("grp"),
        P(),
        P(),
        P(),
        P(),
        P(),
        P(),
    )
    return jax.shard_map(
        local,
        mesh=mesh,
        in_specs=placed,
        out_specs=(P(("grp", "tm"), None, None, None), P(("grp", "tm"), None, None, None)),
        check_vma=False,
    )
```

```python
import functools

import jax
import jax.numpy as jnp
from jax import lax
from jax.experimental import pallas as pl
from jax.experimental.pallas import tpu as pltpu
from jax.sharding import PartitionSpec as P

CH = 16
C = 384
LT = 4
HL = 16
WL = 24
TILE_X = 8
ROWS = HL * WL // TILE_X
PIX = HL * WL
HALO = 2
NF = LT + HALO
K2 = 9 * C
F32 = jnp.float32
BF16 = jnp.bfloat16
LANES = (((1,), (1,)), ((), ()))


def iota(shape, dim):
    return lax.broadcasted_iota(jnp.int32, shape, dim)


def fdiv(x, n):
    return jnp.floor((x + 0.5) * (1.0 / n))


def chunk_sizes(n, tiles):
    cap = max(2, 2 * tiles // n)
    sent = (2 * cap + 8) // 8 * 8
    rows = 8
    while rows < sent:
        rows *= 2
    return cap, sent, rows


def pack_kernel(n, cap, sent, rows, tiles_ref, idx_ref, out_ref):
    tiles = tiles_ref.shape[0]
    ids = idx_ref[...].astype(F32)
    r_row = fdiv(ids, tiles)
    s_row = ids - r_row * tiles
    sub = iota((tiles, tiles), 0)
    lane = iota((tiles, tiles), 1)
    r_col = jnp.sum(jnp.where(sub == lane, r_row, 0.0), axis=1, keepdims=True)
    same = r_col == r_row
    rank_row = jnp.sum(jnp.where(same & (sub < lane), 1.0, 0.0), axis=0, keepdims=True)
    rank_col = jnp.sum(jnp.where(same & (lane < sub), 1.0, 0.0), axis=1, keepdims=True)
    pos_row = r_row * cap + rank_row
    rho = iota((n * sent, 1), 0).astype(F32)
    d = fdiv(rho, sent)
    q = rho - d * sent
    key = jnp.where(q < cap, d * cap + q, jnp.where(q < 2 * cap, (d - 1.0) * cap + q - cap, -1.0))
    onehot = (key == pos_row).astype(F32).astype(BF16)
    moved = jnp.dot(onehot, tiles_ref[...].astype(BF16), preferred_element_type=F32)
    dev = iota((n, 1), 0).astype(F32)
    slot1 = s_row + 1.0
    a_own = jnp.where(dev == r_row, slot1, 0.0).astype(BF16)
    a_prev = jnp.where(dev - 1.0 == r_row, slot1, 0.0).astype(BF16)
    offset = lax.rem(lax.axis_index("tm"), 128 // rows) * rows
    place = iota((tiles, 128), 1) - offset
    rank_i = rank_col.astype(jnp.int32)
    b_own = (place == rank_i).astype(F32).astype(BF16)
    b_prev = (place - cap == rank_i).astype(F32).astype(BF16)
    id_rows = jnp.dot(a_own, b_own, preferred_element_type=F32) + jnp.dot(
        a_prev, b_prev, preferred_element_type=F32
    )
    q3 = iota((n, sent, 128), 1)
    full = jnp.where(q3 == 2 * cap, id_rows[:, None, :], moved.reshape(n, sent, 128))
    out_ref[...] = full.astype(BF16)


def pair_kernel(w1_ref, wp_ref):
    zero = jnp.zeros((CH, C), BF16)
    for d in range(3):
        for a in range(3):
            for c in range(4):
                for j in range(2):
                    rows = pl.ds((3 * d + a) * 64 + c * CH, CH)
                    inside = 0 <= c - j < 3
                    value = w1_ref[d, pl.ds((3 * a + c - j) * CH, CH), :].astype(BF16) if inside else zero
                    wp_ref[rows, pl.ds(j * C, C)] = value


def mix_kernel(w2_ref, ut_ref, w2v, utv, sem):
    kb = 3 * C

    def fetch(d, a):
        part = pl.ds(a * kb, kb)
        return pltpu.make_async_copy(w2_ref.at[d, part, :], w2v.at[d, part, :], sem.at[3 * d + a])

    def put(d):
        part = pl.ds(d * kb, kb)
        return pltpu.make_async_copy(utv.at[:, :, part], ut_ref.at[:, :, part], sem.at[9 + d])

    for d in range(3):
        for a in range(3):
            fetch(d, a).start()
    eye = (iota((C, C), 0) == iota((C, C), 1)).astype(F32).astype(BF16)
    for d in range(3):
        for a in range(3):
            fetch(d, a).wait()
        for n0 in range(0, kb, 256):
            wide = min(256, kb - n0)
            g = [
                lax.dot_general(
                    eye, w2v[d, pl.ds(a * kb + n0, wide), :], LANES, preferred_element_type=F32
                )
                for a in range(3)
            ]
            outer = g[0] + g[2]
            at = pl.ds(d * kb + n0, wide)
            for k, value in enumerate((g[0], 0.5 * (outer + g[1]), 0.5 * (outer - g[1]), g[2])):
                utv[k, :, at] = value.astype(BF16)
        put(d).start()
    for d in range(3):
        put(d).wait()


def activate(values, half_gain):
    ms = jnp.mean(values * values, axis=-1, keepdims=True)
    scaled = values * lax.rsqrt(ms + 1e-06) * half_gain
    return scaled + scaled * jnp.tanh(scaled)


def decode_kernel(
    cap,
    vfc_ref,
    inc_ref,
    wp_ref,
    b1_ref,
    g1_ref,
    ut_ref,
    b2_ref,
    g2_ref,
    bi_ref,
    ba_ref,
    inc_v,
    utv,
    win,
    lhs,
    pre_early,
    pre_late,
    actf_even,
    actf_odd,
    mixed,
    sums,
    turned,
    columns,
    bi_v,
    ba_v,
    sem,
):
    n, sent, _ = inc_ref.shape
    actf = (actf_even, actf_odd)

    def load(k):
        return pltpu.make_async_copy(ut_ref.at[k], utv.at[k], sem.at[1 + 2 * LT + k])

    for k in range(4):
        load(k).start()

    rows = inc_v.shape[1]
    inc_v[:, :sent, :] = inc_ref[...]
    if rows > sent:
        inc_v[:, sent:, :] = jnp.zeros((n, rows - sent, 128), BF16)

    def send(source, target, o, first_sem):
        return pltpu.make_async_copy(
            source.at[o], target.at[pl.ds(o * PIX, PIX), :], sem.at[first_sem + o]
        )

    bias1, gain1 = b1_ref[...].reshape(1, C), 0.5 * g1_ref[...].reshape(1, C)
    diagonal = iota((C, C), 0) == iota((C, C), 1)
    for k, ref in enumerate((b2_ref, g2_ref)):
        column = jnp.sum(jnp.where(diagonal, ref[...].reshape(1, C), 0.0), axis=1, keepdims=True)
        columns[k] = jnp.broadcast_to(column * (0.5 if k else 1.0), (C, 128))
    first = lax.axis_index("tm") * LT
    starts = [jnp.int32(0)] * NF
    bound = jnp.int32(0)
    for v in range(vfc_ref.shape[0]):
        for f in range(NF):
            starts[f] = jnp.where(bound <= first - HALO + f, bound, starts[f])
        bound = bound + vfc_ref[v]
    lags = []
    for f in range(NF):
        t = first - HALO + f
        lags.append(
            [
                None,
                jnp.where(t - 1 >= starts[f], 1.0, 0.0).astype(F32),
                jnp.where(t - 2 >= starts[f], 1.0, 0.0).astype(F32),
            ]
        )
    total = n * rows
    groups = total // 128
    inc = inc_v[...].reshape(total, 128)
    k_idx = iota((8, total), 1)
    sel = (lax.rem(k_idx, rows) == 2 * cap) & (lax.div(k_idx, 128) == iota((8, total), 0))
    ids = jnp.dot(sel.astype(F32).astype(BF16), inc, preferred_element_type=F32)
    place = lax.rem(iota((1, 128), 1), rows)
    half = LT * ROWS
    slot1 = (iota((half, 1), 0) + 1).astype(F32)
    pieces = []
    for g in range(groups):
        id_g = ids[g : g + 1, :]
        own = jnp.where(place < cap, id_g, 0.0)
        prev = jnp.where((place >= cap) & (place < 2 * cap), id_g, 0.0)
        hit = jnp.concatenate([slot1 == prev, slot1 == own], axis=0)
        pieces.append(hit.astype(F32).astype(BF16))
    tiles = jnp.dot(jnp.concatenate(pieces, axis=1), inc, preferred_element_type=F32)
    n_rows = 2 * half
    step = WL // TILE_X
    rho = iota((n_rows, 1), 0).astype(F32)
    xt = rho - fdiv(rho, step) * step
    lane = iota((n_rows, 128), 1)
    left = jnp.where(xt >= 1, pltpu.roll(tiles, 1, 0), 0.0)
    right = jnp.where(xt <= step - 2, pltpu.roll(tiles, n_rows - 1, 0), 0.0)
    y = jnp.where(lane < CH, pltpu.roll(left, CH, 1), pltpu.roll(tiles, CH, 1))
    z = jnp.where(lane < 3 * CH, pltpu.roll(tiles, 3 * CH, 1), pltpu.roll(right, 3 * CH, 1))
    middle = pl.ds(8, n_rows)
    for k, value in enumerate(
        (y, pltpu.roll(y, 96, 1), pltpu.roll(y, 64, 1), pltpu.roll(y, 32, 1), z, pltpu.roll(z, 64, 1))
    ):
        win[k, pl.ds(0, 8), :] = jnp.zeros((8, 128), F32)
        win[k, pl.ds(8 + n_rows, 8), :] = jnp.zeros((8, 128), F32)
        win[k, middle, :] = value
    low = (0, 1, 2, 4)
    high = (2, 3, 0, 5)
    lane48 = iota((ROWS, 128), 1)
    row48 = iota((ROWS, 128), 0)
    inside = (
        jnp.where(row48 >= step, 1.0, 0.0),
        None,
        jnp.where(row48 < ROWS - step, 1.0, 0.0),
    )

    def tap_rows(tap, which, f):
        d, a = divmod(tap, 3)
        value = win[which, pl.ds(8 + (f + HALO - d) * ROWS + step * (a - 1), ROWS), :]
        if a != 1:
            value = value * inside[a]
        return value if d == 0 else value * lags[f][d]

    def lhs_piece(p, f):
        for m in range(5):
            value = tap_rows(2 * m, low[p], f)
            if m < 4:
                value = jnp.where(lane48 < 64, value, tap_rows(2 * m + 1, high[p], f))
            lhs[p, pl.ds(f * ROWS, ROWS), pl.ds(m * 128, 128)] = value.astype(BF16)

    def first_piece(p, f0, f1):
        rows_f = pl.ds(f0 * ROWS, (f1 - f0) * ROWS)
        out = jnp.dot(lhs[p, rows_f, : 9 * 64], wp_ref[...], preferred_element_type=F32)
        for j in range(2 * C // 128):
            x_col, m = 2 * p + j // 3, j % 3
            target = pl.ds(x_col, (f1 - f0) * ROWS, stride=TILE_X)
            pre = pre_late if f0 else pre_early
            pre[m, target, :] = out[:, j * 128 : (j + 1) * 128]

    act_rows = 2 * WL
    base = 8
    gap = WL + 8
    pairs = HL // 2
    half_pix = PIX // 2
    some = pairs // 2
    kb = 3 * C
    for ref in actf:
        for h in (0, HL + 1):
            ref[pl.ds(base + h * gap, WL), :] = jnp.zeros((WL, C), F32)
        for h in range(HL + 3):
            ref[pl.ds(h * gap, base), :] = jnp.zeros((base, C), F32)

    def act_piece(f, r):
        pre, at = (pre_early, f) if f < HALO else (pre_late, f - HALO)
        rows_r = pl.ds(at * PIX + r * act_rows, act_rows)
        raw = jnp.concatenate([pre[m, rows_r, :] for m in range(3)], axis=1)
        block = (raw + bias1).astype(BF16)
        if f >= HALO:
            bi_v[f - HALO, pl.ds(r * act_rows, act_rows), :] = block
        value = activate(block.astype(F32), gain1)
        for t in range(2):
            at = pl.ds(base + (2 * r + t + 1) * gap, WL)
            actf[f % 2][at, :] = value[t * WL : (t + 1) * WL]

    def mix_piece(f, i0, m):
        lanes = pl.ds(m * 128, 128)
        for b in range(3):
            rows_h = [
                actf[f % 2][pl.ds(base + (2 * i0 + h) * gap + b - 1, WL), lanes]
                for h in range(2 * some + 2)
            ]
            d0, d1, d2, d3 = (
                jnp.concatenate([rows_h[2 * i + h] for i in range(some)], axis=0) for h in range(4)
            )
            at = pl.ds(b * C + m * 128, 128)
            for k, value in enumerate((d0 - d2, d1 + d2, d2 - d1, d1 - d3)):
                mixed[k, pl.ds(f * half_pix + i0 * WL, some * WL), at] = value.astype(BF16)

    def frame_work(f):
        work = [functools.partial(act_piece, f, r) for r in range(PIX // act_rows)]
        for i0 in range(0, pairs, some):
            work += [functools.partial(mix_piece, f, i0, m) for m in range(3)]
        return work

    def lag_lanes(d, j):
        pixel = iota((1, 256), 1) + j * 256
        value = jnp.zeros((1, 256), F32)
        for o in range(LT):
            here = (pixel >= o * half_pix) & (pixel < (o + 1) * half_pix)
            value = jnp.where(here, lags[o + HALO][d], value)
        return value

    def mxu_piece(d, j, k):
        if d == 2 and j == 0:
            load(k).wait()
        rows_p = pl.ds((HALO - d) * half_pix + j * 256, 256)
        prod = lax.dot_general(
            utv[k, :, d * kb : (d + 1) * kb], mixed[k, rows_p, :], LANES, preferred_element_type=F32
        )
        if d > 0:
            prod = prod * lag_lanes(d, j)
        at = pl.ds(j * 256, 256)
        if k < 3:
            sums[0, :, at] = prod if d == 2 and k == 0 else sums[0, :, at] + prod
        if k == 1:
            sums[1, :, at] = prod if d == 2 else sums[1, :, at] + prod
        if k > 1:
            sums[1, :, at] = sums[1, :, at] - prod

    def norm_piece(part, lb):
        lanes = pl.ds(lb * 128, 128)
        blocks = [pl.ds(c * 128, 128) for c in range(C // 128)]
        total_sq = jnp.zeros((1, 128), F32)
        for rows_c in blocks:
            value = sums[part, rows_c, lanes] + columns[0, rows_c, :]
            total_sq = total_sq + jnp.sum(value * value, axis=0, keepdims=True)
        scale = lax.rsqrt(total_sq * (1.0 / C) + 1e-06)
        for rows_c in blocks:
            value = (sums[part, rows_c, lanes] + columns[0, rows_c, :]) * scale * columns[1, rows_c, :]
            value = value + value * jnp.tanh(value)
            turned[part, lanes, rows_c] = value.T

    def store_piece(pair):
        o, i = divmod(pair, pairs)
        rows_i = pl.ds(pair * WL, WL)
        both = jnp.concatenate([turned[0, rows_i, :], turned[1, rows_i, :]], axis=0)
        ba_v[o, pl.ds(i * 2 * WL, 2 * WL), :] = both.astype(BF16)

    def end_work(j):
        work = [
            functools.partial(norm_piece, part, lb)
            for lb in (2 * j, 2 * j + 1)
            for part in range(2)
        ]
        return work + [
            functools.partial(store_piece, pair)
            for pair in range(256 * j // WL, 256 * (j + 1) // WL)
        ]

    def weave(work, pieces):
        given = 0
        for i, piece in enumerate(pieces):
            upto = len(work) * (i + 1) // len(pieces)
            for vector_piece in work[given:upto]:
                vector_piece()
            given = upto
            piece()

    early = HALO
    for p in range(4):
        for f in range(early):
            lhs_piece(p, f)
    weave(
        [functools.partial(lhs_piece, p, f) for p in range(4) for f in range(early, NF)],
        [functools.partial(first_piece, p, 0, early) for p in range(4)],
    )
    weave(
        frame_work(0) + frame_work(1),
        [functools.partial(first_piece, p, early, NF) for p in range(4)],
    )
    stages = (
        (((2, 0),), frame_work(2)),
        (((2, 1), (1, 0)), frame_work(3)),
        (((2, 2), (1, 1), (0, 0)), frame_work(4)),
        (((1, 2), (0, 1)), frame_work(5) + end_work(0)),
        (((0, 2),), end_work(1)),
    )
    for s, (tiles_s, work) in enumerate(stages):
        pieces = [functools.partial(mxu_piece, d, j, k) for d, j in tiles_s for k in range(4)]
        weave(work, pieces)
        if s == 3:
            for o in range(LT):
                send(bi_v, bi_ref, o, 1).start()
            send(ba_v, ba_ref, 0, 1 + LT).start()
        if s == 4:
            send(ba_v, ba_ref, 1, 1 + LT).start()
    for piece in end_work(2):
        piece()
    for o in (2, 3):
        send(ba_v, ba_ref, o, 1 + LT).start()
    for o in range(LT):
        send(bi_v, bi_ref, o, 1).wait()
        send(ba_v, ba_ref, o, 1 + LT).wait()


def local(
    transformer_tiles,
    global_tile_index,
    video_frame_count,
    input_conv_weight,
    input_conv_bias,
    first_norm_gain,
    residual_conv_weight,
    residual_conv_bias,
    second_norm_gain,
):
    n = lax.axis_size("tm")
    cap, sent, rows = chunk_sizes(n, transformer_tiles.shape[0])
    vmem = pl.BlockSpec(memory_space=pltpu.VMEM)
    smem = pl.BlockSpec(memory_space=pltpu.SMEM)
    hbm = pl.BlockSpec(memory_space=pltpu.HBM)
    outbound = pl.pallas_call(
        functools.partial(pack_kernel, n, cap, sent, rows),
        out_shape=jax.ShapeDtypeStruct((n, sent, 128), BF16),
        in_specs=[vmem, vmem],
        out_specs=vmem,
        name="pack",
    )(transformer_tiles, global_tile_index)
    incoming = lax.all_to_all(outbound, "tm", split_axis=0, concat_axis=0, tiled=True)
    pair_weights = pl.pallas_call(
        pair_kernel,
        out_shape=pltpu.VMEM((9 * 64, 2 * C), BF16),
        in_specs=[vmem],
        out_specs=vmem,
        compiler_params=pltpu.CompilerParams(vmem_limit_bytes=16 << 20),
        name="pair",
    )(input_conv_weight)
    mixed_weights = pl.pallas_call(
        mix_kernel,
        out_shape=jax.ShapeDtypeStruct((4, C, K2), BF16),
        in_specs=[hbm],
        out_specs=hbm,
        scratch_shapes=[
            pltpu.VMEM((3, K2, C), BF16),
            pltpu.VMEM((4, C, K2), BF16),
            pltpu.SemaphoreType.DMA((12,)),
        ],
        compiler_params=pltpu.CompilerParams(vmem_limit_bytes=57 << 20),
        name="mix",
    )(residual_conv_weight)
    half = LT * ROWS
    block_input, branch_act = pl.pallas_call(
        functools.partial(decode_kernel, cap),
        out_shape=[jax.ShapeDtypeStruct((LT * PIX, C), BF16)] * 2,
        in_specs=[smem, vmem, vmem, vmem, vmem, hbm, vmem, vmem],
        out_specs=[hbm, hbm],
        scratch_shapes=[
            pltpu.VMEM((n, rows, 128), BF16),
            pltpu.VMEM((4, C, K2), BF16),
            pltpu.VMEM((6, 2 * half + 16, 128), F32),
            pltpu.VMEM((4, NF * ROWS, 640), BF16),
            pltpu.VMEM((3, HALO * PIX, 128), F32),
            pltpu.VMEM((3, LT * PIX, 128), F32),
            pltpu.VMEM(((HL + 3) * (WL + 8), C), F32),
            pltpu.VMEM(((HL + 3) * (WL + 8), C), F32),
            pltpu.VMEM((4, NF * PIX // 2, 3 * C), BF16),
            pltpu.VMEM((2, C, LT * PIX // 2), F32),
            pltpu.VMEM((2, LT * PIX // 2, C), F32),
            pltpu.VMEM((2, C, 128), F32),
            pltpu.VMEM((LT, PIX, C), BF16),
            pltpu.VMEM((LT, PIX, C), BF16),
            pltpu.SemaphoreType.DMA((1 + 2 * LT + 4,)),
        ],
        compiler_params=pltpu.CompilerParams(vmem_limit_bytes=48 << 20),
        name="decode",
    )(
        video_frame_count,
        incoming,
        pair_weights,
        input_conv_bias,
        first_norm_gain,
        mixed_weights,
        residual_conv_bias,
        second_norm_gain,
    )
    shape = (LT, HL, WL, C)
    return (block_input.reshape(shape), branch_act.reshape(shape))


def solution(mesh):
    placed = (
        P(("grp", "tm"), None),
        P(("grp", "tm"), None),
        P("grp"),
        P(),
        P(),
        P(),
        P(),
        P(),
        P(),
    )
    return jax.shard_map(
        local,
        mesh=mesh,
        in_specs=placed,
        out_specs=(P(("grp", "tm"), None, None, None), P(("grp", "tm"), None, None, None)),
        check_vma=False,
    )
```

```python
import functools

import jax
import jax.numpy as jnp
from jax import lax
from jax.experimental import pallas as pl
from jax.experimental.pallas import tpu as pltpu
from jax.sharding import PartitionSpec as P

CH = 16
C = 384
LT = 4
HL = 16
WL = 24
TILE_X = 8
ROWS = HL * WL // TILE_X
PIX = HL * WL
HALO = 2
NF = LT + HALO
K2 = 9 * C
F32 = jnp.float32
BF16 = jnp.bfloat16
LANES = (((1,), (1,)), ((), ()))


def iota(shape, dim):
    return lax.broadcasted_iota(jnp.int32, shape, dim)


def fdiv(x, n):
    return jnp.floor((x + 0.5) * (1.0 / n))


def chunk_sizes(n, tiles):
    cap = max(2, 2 * tiles // n)
    sent = (2 * cap + 8) // 8 * 8
    rows = 8
    while rows < sent:
        rows *= 2
    return cap, sent, rows


def pack_kernel(n, cap, sent, rows, tiles_ref, idx_ref, out_ref):
    tiles = tiles_ref.shape[0]
    ids = idx_ref[...].astype(F32)
    r_row = fdiv(ids, tiles)
    s_row = ids - r_row * tiles
    sub = iota((tiles, tiles), 0)
    lane = iota((tiles, tiles), 1)
    r_col = jnp.sum(jnp.where(sub == lane, r_row, 0.0), axis=1, keepdims=True)
    same = r_col == r_row
    rank_row = jnp.sum(jnp.where(same & (sub < lane), 1.0, 0.0), axis=0, keepdims=True)
    rank_col = jnp.sum(jnp.where(same & (lane < sub), 1.0, 0.0), axis=1, keepdims=True)
    pos_row = r_row * cap + rank_row
    rho = iota((n * sent, 1), 0).astype(F32)
    d = fdiv(rho, sent)
    q = rho - d * sent
    key = jnp.where(q < cap, d * cap + q, jnp.where(q < 2 * cap, (d - 1.0) * cap + q - cap, -1.0))
    onehot = (key == pos_row).astype(F32).astype(BF16)
    moved = jnp.dot(onehot, tiles_ref[...].astype(BF16), preferred_element_type=F32)
    dev = iota((n, 1), 0).astype(F32)
    slot1 = s_row + 1.0
    a_own = jnp.where(dev == r_row, slot1, 0.0).astype(BF16)
    a_prev = jnp.where(dev - 1.0 == r_row, slot1, 0.0).astype(BF16)
    offset = lax.rem(lax.axis_index("tm"), 128 // rows) * rows
    place = iota((tiles, 128), 1) - offset
    rank_i = rank_col.astype(jnp.int32)
    b_own = (place == rank_i).astype(F32).astype(BF16)
    b_prev = (place - cap == rank_i).astype(F32).astype(BF16)
    id_rows = jnp.dot(a_own, b_own, preferred_element_type=F32) + jnp.dot(
        a_prev, b_prev, preferred_element_type=F32
    )
    q3 = iota((n, sent, 128), 1)
    full = jnp.where(q3 == 2 * cap, id_rows[:, None, :], moved.reshape(n, sent, 128))
    out_ref[...] = full.astype(BF16)


def build_pairs(w1_ref, wp_ref):
    zero = jnp.zeros((CH, C), BF16)
    for d in range(3):
        for a in range(3):
            for c in range(4):
                for j in range(2):
                    rows = pl.ds((3 * d + a) * 64 + c * CH, CH)
                    inside = 0 <= c - j < 3
                    value = w1_ref[d, pl.ds((3 * a + c - j) * CH, CH), :].astype(BF16) if inside else zero
                    wp_ref[rows, pl.ds(j * C, C)] = value


def mix_kernel(w2_ref, ut_ref, w2v, utv, sem):
    kb = 3 * C

    def fetch(d, a):
        part = pl.ds(a * kb, kb)
        return pltpu.make_async_copy(w2_ref.at[d, part, :], w2v.at[d, part, :], sem.at[3 * d + a])

    def put(d):
        part = pl.ds(d * kb, kb)
        return pltpu.make_async_copy(utv.at[:, :, part], ut_ref.at[:, :, part], sem.at[9 + d])

    for d in range(3):
        for a in range(3):
            fetch(d, a).start()
    eye = (iota((C, C), 0) == iota((C, C), 1)).astype(F32).astype(BF16)
    for d in range(3):
        for a in range(3):
            fetch(d, a).wait()
        for n0 in range(0, kb, 256):
            wide = min(256, kb - n0)
            g = [
                lax.dot_general(
                    eye, w2v[d, pl.ds(a * kb + n0, wide), :], LANES, preferred_element_type=F32
                )
                for a in range(3)
            ]
            outer = g[0] + g[2]
            at = pl.ds(d * kb + n0, wide)
            for k, value in enumerate((g[0], 0.5 * (outer + g[1]), 0.5 * (outer - g[1]), g[2])):
                utv[k, :, at] = value.astype(BF16)
        put(d).start()
    for d in range(3):
        put(d).wait()


def activate(values, half_gain):
    ms = jnp.mean(values * values, axis=-1, keepdims=True)
    scaled = values * lax.rsqrt(ms + 1e-06) * half_gain
    return scaled + scaled * jnp.tanh(scaled)


def decode_kernel(
    cap,
    vfc_ref,
    inc_ref,
    w1_ref,
    b1_ref,
    g1_ref,
    ut_ref,
    b2_ref,
    g2_ref,
    bi_ref,
    ba_ref,
    inc_v,
    wp_ref,
    utv,
    win,
    lhs,
    pre_early,
    pre_late,
    actf_even,
    actf_odd,
    mixed,
    sums,
    turned,
    columns,
    bi_v,
    ba_v,
    sem,
):
    n, sent, _ = inc_ref.shape
    actf = (actf_even, actf_odd)

    def load(k):
        return pltpu.make_async_copy(ut_ref.at[k], utv.at[k], sem.at[1 + 2 * LT + k])

    for k in range(4):
        load(k).start()

    build_pairs(w1_ref, wp_ref)
    rows = inc_v.shape[1]
    inc_v[:, :sent, :] = inc_ref[...]
    if rows > sent:
        inc_v[:, sent:, :] = jnp.zeros((n, rows - sent, 128), BF16)

    def send(source, target, o, first_sem):
        return pltpu.make_async_copy(
            source.at[o], target.at[pl.ds(o * PIX, PIX), :], sem.at[first_sem + o]
        )

    bias1, gain1 = b1_ref[...].reshape(1, C), 0.5 * g1_ref[...].reshape(1, C)
    diagonal = iota((C, C), 0) == iota((C, C), 1)
    for k, ref in enumerate((b2_ref, g2_ref)):
        column = jnp.sum(jnp.where(diagonal, ref[...].reshape(1, C), 0.0), axis=1, keepdims=True)
        columns[k] = jnp.broadcast_to(column * (0.5 if k else 1.0), (C, 128))
    first = lax.axis_index("tm") * LT
    starts = [jnp.int32(0)] * NF
    bound = jnp.int32(0)
    for v in range(vfc_ref.shape[0]):
        for f in range(NF):
            starts[f] = jnp.where(bound <= first - HALO + f, bound, starts[f])
        bound = bound + vfc_ref[v]
    lags = []
    for f in range(NF):
        t = first - HALO + f
        lags.append(
            [
                None,
                jnp.where(t - 1 >= starts[f], 1.0, 0.0).astype(F32),
                jnp.where(t - 2 >= starts[f], 1.0, 0.0).astype(F32),
            ]
        )
    total = n * rows
    groups = total // 128
    inc = inc_v[...].reshape(total, 128)
    k_idx = iota((8, total), 1)
    sel = (lax.rem(k_idx, rows) == 2 * cap) & (lax.div(k_idx, 128) == iota((8, total), 0))
    ids = jnp.dot(sel.astype(F32).astype(BF16), inc, preferred_element_type=F32)
    place = lax.rem(iota((1, 128), 1), rows)
    half = LT * ROWS
    slot1 = (iota((half, 1), 0) + 1).astype(F32)
    pieces = []
    for g in range(groups):
        id_g = ids[g : g + 1, :]
        own = jnp.where(place < cap, id_g, 0.0)
        prev = jnp.where((place >= cap) & (place < 2 * cap), id_g, 0.0)
        hit = jnp.concatenate([slot1 == prev, slot1 == own], axis=0)
        pieces.append(hit.astype(F32).astype(BF16))
    tiles = jnp.dot(jnp.concatenate(pieces, axis=1), inc, preferred_element_type=F32)
    n_rows = 2 * half
    step = WL // TILE_X
    rho = iota((n_rows, 1), 0).astype(F32)
    xt = rho - fdiv(rho, step) * step
    lane = iota((n_rows, 128), 1)
    left = jnp.where(xt >= 1, pltpu.roll(tiles, 1, 0), 0.0)
    right = jnp.where(xt <= step - 2, pltpu.roll(tiles, n_rows - 1, 0), 0.0)
    y = jnp.where(lane < CH, pltpu.roll(left, CH, 1), pltpu.roll(tiles, CH, 1))
    z = jnp.where(lane < 3 * CH, pltpu.roll(tiles, 3 * CH, 1), pltpu.roll(right, 3 * CH, 1))
    middle = pl.ds(8, n_rows)
    for k, value in enumerate(
        (y, pltpu.roll(y, 96, 1), pltpu.roll(y, 64, 1), pltpu.roll(y, 32, 1), z, pltpu.roll(z, 64, 1))
    ):
        win[k, pl.ds(0, 8), :] = jnp.zeros((8, 128), F32)
        win[k, pl.ds(8 + n_rows, 8), :] = jnp.zeros((8, 128), F32)
        win[k, middle, :] = value
    low = (0, 1, 2, 4)
    high = (2, 3, 0, 5)
    lane48 = iota((ROWS, 128), 1)
    row48 = iota((ROWS, 128), 0)
    inside = (
        jnp.where(row48 >= step, 1.0, 0.0),
        None,
        jnp.where(row48 < ROWS - step, 1.0, 0.0),
    )

    def tap_rows(tap, which, f):
        d, a = divmod(tap, 3)
        value = win[which, pl.ds(8 + (f + HALO - d) * ROWS + step * (a - 1), ROWS), :]
        if a != 1:
            value = value * inside[a]
        return value if d == 0 else value * lags[f][d]

    def lhs_piece(p, f):
        for m in range(5):
            value = tap_rows(2 * m, low[p], f)
            if m < 4:
                value = jnp.where(lane48 < 64, value, tap_rows(2 * m + 1, high[p], f))
            lhs[p, pl.ds(f * ROWS, ROWS), pl.ds(m * 128, 128)] = value.astype(BF16)

    def first_piece(p, f0, f1):
        rows_f = pl.ds(f0 * ROWS, (f1 - f0) * ROWS)
        out = jnp.dot(lhs[p, rows_f, : 9 * 64], wp_ref[...], preferred_element_type=F32)
        for j in range(2 * C // 128):
            x_col, m = 2 * p + j // 3, j % 3
            target = pl.ds(x_col, (f1 - f0) * ROWS, stride=TILE_X)
            pre = pre_late if f0 else pre_early
            pre[m, target, :] = out[:, j * 128 : (j + 1) * 128]

    act_rows = 2 * WL
    base = 8
    gap = WL + 8
    pairs = HL // 2
    half_pix = PIX // 2
    some = pairs // 2
    kb = 3 * C
    for ref in actf:
        for h in (0, HL + 1):
            ref[pl.ds(base + h * gap, WL), :] = jnp.zeros((WL, C), F32)
        for h in range(HL + 3):
            ref[pl.ds(h * gap, base), :] = jnp.zeros((base, C), F32)

    def act_piece(f, r):
        pre, at = (pre_early, f) if f < HALO else (pre_late, f - HALO)
        rows_r = pl.ds(at * PIX + r * act_rows, act_rows)
        raw = jnp.concatenate([pre[m, rows_r, :] for m in range(3)], axis=1)
        block = (raw + bias1).astype(BF16)
        if f >= HALO:
            bi_v[f - HALO, pl.ds(r * act_rows, act_rows), :] = block
        value = activate(block.astype(F32), gain1)
        for t in range(2):
            at = pl.ds(base + (2 * r + t + 1) * gap, WL)
            actf[f % 2][at, :] = value[t * WL : (t + 1) * WL]

    def mix_piece(f, i0, m):
        lanes = pl.ds(m * 128, 128)
        for b in range(3):
            rows_h = [
                actf[f % 2][pl.ds(base + (2 * i0 + h) * gap + b - 1, WL), lanes]
                for h in range(2 * some + 2)
            ]
            d0, d1, d2, d3 = (
                jnp.concatenate([rows_h[2 * i + h] for i in range(some)], axis=0) for h in range(4)
            )
            at = pl.ds(b * C + m * 128, 128)
            for k, value in enumerate((d0 - d2, d1 + d2, d2 - d1, d1 - d3)):
                mixed[k, pl.ds(f * half_pix + i0 * WL, some * WL), at] = value.astype(BF16)

    def frame_work(f):
        work = [functools.partial(act_piece, f, r) for r in range(PIX // act_rows)]
        for i0 in range(0, pairs, some):
            work += [functools.partial(mix_piece, f, i0, m) for m in range(3)]
        return work

    def lag_lanes(d, j):
        pixel = iota((1, 256), 1) + j * 256
        value = jnp.zeros((1, 256), F32)
        for o in range(LT):
            here = (pixel >= o * half_pix) & (pixel < (o + 1) * half_pix)
            value = jnp.where(here, lags[o + HALO][d], value)
        return value

    def mxu_piece(d, j, k):
        if d == 2 and j == 0:
            load(k).wait()
        rows_p = pl.ds((HALO - d) * half_pix + j * 256, 256)
        prod = lax.dot_general(
            utv[k, :, d * kb : (d + 1) * kb], mixed[k, rows_p, :], LANES, preferred_element_type=F32
        )
        if d > 0:
            prod = prod * lag_lanes(d, j)
        at = pl.ds(j * 256, 256)
        if k < 3:
            sums[0, :, at] = prod if d == 2 and k == 0 else sums[0, :, at] + prod
        if k == 1:
            sums[1, :, at] = prod if d == 2 else sums[1, :, at] + prod
        if k > 1:
            sums[1, :, at] = sums[1, :, at] - prod

    def norm_piece(part, lb):
        lanes = pl.ds(lb * 128, 128)
        blocks = [pl.ds(c * 128, 128) for c in range(C // 128)]
        total_sq = jnp.zeros((1, 128), F32)
        for rows_c in blocks:
            value = sums[part, rows_c, lanes] + columns[0, rows_c, :]
            total_sq = total_sq + jnp.sum(value * value, axis=0, keepdims=True)
        scale = lax.rsqrt(total_sq * (1.0 / C) + 1e-06)
        for rows_c in blocks:
            value = (sums[part, rows_c, lanes] + columns[0, rows_c, :]) * scale * columns[1, rows_c, :]
            value = value + value * jnp.tanh(value)
            turned[part, lanes, rows_c] = value.T

    def store_piece(pair):
        o, i = divmod(pair, pairs)
        rows_i = pl.ds(pair * WL, WL)
        both = jnp.concatenate([turned[0, rows_i, :], turned[1, rows_i, :]], axis=0)
        ba_v[o, pl.ds(i * 2 * WL, 2 * WL), :] = both.astype(BF16)

    def end_work(j):
        work = [
            functools.partial(norm_piece, part, lb)
            for lb in (2 * j, 2 * j + 1)
            for part in range(2)
        ]
        return work + [
            functools.partial(store_piece, pair)
            for pair in range(256 * j // WL, 256 * (j + 1) // WL)
        ]

    def weave(work, pieces):
        given = 0
        for i, piece in enumerate(pieces):
            upto = len(work) * (i + 1) // len(pieces)
            for vector_piece in work[given:upto]:
                vector_piece()
            given = upto
            piece()

    early = HALO
    for p in range(4):
        for f in range(early):
            lhs_piece(p, f)
    weave(
        [functools.partial(lhs_piece, p, f) for p in range(4) for f in range(early, NF)],
        [functools.partial(first_piece, p, 0, early) for p in range(4)],
    )
    weave(
        frame_work(0) + frame_work(1),
        [functools.partial(first_piece, p, early, NF) for p in range(4)],
    )
    stages = (
        (((2, 0),), frame_work(2)),
        (((2, 1), (1, 0)), frame_work(3)),
        (((2, 2), (1, 1), (0, 0)), frame_work(4)),
        (((1, 2), (0, 1)), frame_work(5) + end_work(0)),
        (((0, 2),), end_work(1)),
    )
    for s, (tiles_s, work) in enumerate(stages):
        pieces = [functools.partial(mxu_piece, d, j, k) for d, j in tiles_s for k in range(4)]
        weave(work, pieces)
        if s == 3:
            for o in range(LT):
                send(bi_v, bi_ref, o, 1).start()
            send(ba_v, ba_ref, 0, 1 + LT).start()
        if s == 4:
            send(ba_v, ba_ref, 1, 1 + LT).start()
    for piece in end_work(2):
        piece()
    for o in (2, 3):
        send(ba_v, ba_ref, o, 1 + LT).start()
    for o in range(LT):
        send(bi_v, bi_ref, o, 1).wait()
        send(ba_v, ba_ref, o, 1 + LT).wait()


def local(
    transformer_tiles,
    global_tile_index,
    video_frame_count,
    input_conv_weight,
    input_conv_bias,
    first_norm_gain,
    residual_conv_weight,
    residual_conv_bias,
    second_norm_gain,
):
    n = lax.axis_size("tm")
    cap, sent, rows = chunk_sizes(n, transformer_tiles.shape[0])
    vmem = pl.BlockSpec(memory_space=pltpu.VMEM)
    smem = pl.BlockSpec(memory_space=pltpu.SMEM)
    hbm = pl.BlockSpec(memory_space=pltpu.HBM)
    outbound = pl.pallas_call(
        functools.partial(pack_kernel, n, cap, sent, rows),
        out_shape=jax.ShapeDtypeStruct((n, sent, 128), BF16),
        in_specs=[vmem, vmem],
        out_specs=vmem,
        name="pack",
    )(transformer_tiles, global_tile_index)
    incoming = lax.all_to_all(outbound, "tm", split_axis=0, concat_axis=0, tiled=True)
    mixed_weights = pl.pallas_call(
        mix_kernel,
        out_shape=jax.ShapeDtypeStruct((4, C, K2), BF16),
        in_specs=[hbm],
        out_specs=hbm,
        scratch_shapes=[
            pltpu.VMEM((3, K2, C), BF16),
            pltpu.VMEM((4, C, K2), BF16),
            pltpu.SemaphoreType.DMA((12,)),
        ],
        compiler_params=pltpu.CompilerParams(vmem_limit_bytes=57 << 20),
        name="mix",
    )(residual_conv_weight)
    half = LT * ROWS
    block_input, branch_act = pl.pallas_call(
        functools.partial(decode_kernel, cap),
        out_shape=[jax.ShapeDtypeStruct((LT * PIX, C), BF16)] * 2,
        in_specs=[smem, vmem, vmem, vmem, vmem, hbm, vmem, vmem],
        out_specs=[hbm, hbm],
        scratch_shapes=[
            pltpu.VMEM((n, rows, 128), BF16),
            pltpu.VMEM((9 * 64, 2 * C), BF16),
            pltpu.VMEM((4, C, K2), BF16),
            pltpu.VMEM((6, 2 * half + 16, 128), F32),
            pltpu.VMEM((4, NF * ROWS, 640), BF16),
            pltpu.VMEM((3, HALO * PIX, 128), F32),
            pltpu.VMEM((3, LT * PIX, 128), F32),
            pltpu.VMEM(((HL + 3) * (WL + 8), C), F32),
            pltpu.VMEM(((HL + 3) * (WL + 8), C), F32),
            pltpu.VMEM((4, NF * PIX // 2, 3 * C), BF16),
            pltpu.VMEM((2, C, LT * PIX // 2), F32),
            pltpu.VMEM((2, LT * PIX // 2, C), F32),
            pltpu.VMEM((2, C, 128), F32),
            pltpu.VMEM((LT, PIX, C), BF16),
            pltpu.VMEM((LT, PIX, C), BF16),
            pltpu.SemaphoreType.DMA((1 + 2 * LT + 4,)),
        ],
        compiler_params=pltpu.CompilerParams(vmem_limit_bytes=48 << 20),
        name="decode",
    )(
        video_frame_count,
        incoming,
        input_conv_weight,
        input_conv_bias,
        first_norm_gain,
        mixed_weights,
        residual_conv_bias,
        second_norm_gain,
    )
    shape = (LT, HL, WL, C)
    return (block_input.reshape(shape), branch_act.reshape(shape))


def solution(mesh):
    placed = (
        P(("grp", "tm"), None),
        P(("grp", "tm"), None),
        P("grp"),
        P(),
        P(),
        P(),
        P(),
        P(),
        P(),
    )
    return jax.shard_map(
        local,
        mesh=mesh,
        in_specs=placed,
        out_specs=(P(("grp", "tm"), None, None, None), P(("grp", "tm"), None, None, None)),
        check_vma=False,
    )
```
